32 devices in a mesh: subj: 2 (over x), row: 8 (over z, y), col: 2 (over core).
Axes of the slice: x: 2, y: 2, z: 4, core: 2. Of those that a mesh axis runs over, the one named last changes fastest.
Arguments:
- bold: bfloat16 [4, 256, 16, 16, 128], P('subj', None, 'row', 'col'), parts along dimension 0, may hold values from -6 to 6
- gm_index: int32 [16384], P(('row', 'col')), may hold values from -1 to 2047, as said below
- partners: int32 [128, 16], P(('row', 'col')), may hold values from -1 to 127, as said below
Outputs:
- connectome: bfloat16 [128, 16, 4, 128, 128], P(('row', 'col'), None, 'subj'), parts along dimension 2
The draws below stay inside these ranges and needn't reach their ends.
There are 2 independent parts, one for each index of `subj`. The reference program is written for one: setup_inputs(seed, part) draws one part's arguments, and reference() takes and returns one part's arrays. A program takes and returns all parts, laid end to end along the dimension named above; an argument that names none is the same for every part. Nothing has to cross between parts.
Inputs may be any that keep to these rules, and one draw needn't show every extreme that they name: `gm_index`: entries of one slab's 1024 rows are distinct voxel numbers, the last few of them -1; every slab has some -1 rows. `partners`: block g lies in slab g // 8, slabs numbered row-major over slab rows and columns. Slot 0 of block i names i, slot 1 names (i + 1) mod 128, slot 2 names (i - 1) mod 128; every named block lies in a slab whose slab row is within 2 of block i's slab row, counted cyclically. -1 marks an empty slot.
All inputs are finite; a program needn't handle non-finite values.
Results may differ from the reference program's by a relative error of at most 0.0053.
Values may be sent and summed in bfloat16 or wider, within the bound.
A program may use at most 128 MiB of HBM per device.

```python
import math
import jax
import jax.numpy as jnp
from jax import lax

W = 2
F = 256
BLOCK = 128
SX = 2
SY = 8
SZ = 128
K = 16
HOP = 2
GROUP = 16
NX = 16
NY = 16
NZ = 128
VLOC = 2048
ROWS_DEV = 1024
NBD = 8
NB = 128
N_ROW = 8
N_COL = 2


def draw_gm_index(key, part):
    slab_keys = jax.random.split(key, GROUP)

    def slab_rows(slab_key):
        first_key, second_key = jax.random.split(slab_key)
        shuffled = jax.random.permutation(first_key, VLOC).astype(jnp.int32)
        chosen = shuffled[:ROWS_DEV]
        spare = shuffled[ROWS_DEV]
        chosen = jnp.where(chosen == VLOC - 1, spare, chosen)
        chosen = chosen.at[0].set(VLOC - 1)
        padding = jax.random.randint(second_key, (), 1, BLOCK // 2 + 1)
        position = jnp.arange(ROWS_DEV).astype(jnp.int32)
        chosen = jnp.where(position >= ROWS_DEV - padding, -1, chosen)
        return chosen.astype(jnp.int32)
    return jax.vmap(slab_rows)(slab_keys).reshape(-1)


def draw_partners(key, part):
    row_key, col_key, block_key, empty_key = jax.random.split(key, 4)
    block_ids = jnp.arange(NB).astype(jnp.int32)
    home_row = block_ids // NBD // N_COL
    offsets = jax.random.randint(row_key, (NB, K), -HOP, HOP + 1)
    target_col = jax.random.randint(col_key, (NB, K), 0, N_COL)
    target_block = jax.random.randint(block_key, (NB, K), 0, NBD)
    target_row = (home_row[:, None] + offsets + N_ROW) % N_ROW
    named = (target_row * N_COL + target_col) * NBD + target_block
    empty = jax.random.randint(empty_key, (NB, K), 0, 4) == 0
    named = jnp.where(empty, -1, named)
    slot = jnp.arange(K).astype(jnp.int32)[None, :]
    named = jnp.where(slot == 0, block_ids[:, None], named)
    named = jnp.where(slot == 1, ((block_ids + 1) % NB)[:, None], named)
    named = jnp.where(slot == 2, ((block_ids - 1 + NB) % NB)[:, None], named)
    named = named.at[0, K - 1].set(-1)
    return named.astype(jnp.int32)


def shard_levels(key, shape, pieces, least, top_value):
    def one(dim, shards_of):
        steps = jax.random.uniform(jax.random.fold_in(jax.random.fold_in(key, 6), dim), (shards_of,), jnp.float32, least / len(pieces), top_value / len(pieces))
        return jnp.repeat(jnp.exp(steps), shape[dim] // shards_of).reshape((-1,) + (1,) * (len(shape) - dim - 1))

    gain = one(*pieces[0])
    for cut in pieces[1:]:
        gain = gain * one(*cut)
    return gain


def gaussian(rng, shape, width, most, shards=(), kind=jnp.bfloat16):
    entries = jax.random.normal(rng, shape, jnp.float32) * width
    if len(shards) > 0:
        entries = shard_levels(rng, shape, shards, -0.22, 0.18) * entries
    return jnp.clip(entries, min=-most, max=most).astype(kind)


def setup_inputs(seed: int = 0, part: int = 0) -> dict:
    seeds = jax.random.split(jax.random.key(seed), 4)
    own_keys = jax.random.split(jax.random.fold_in(seeds[3], part), 4)
    bold = gaussian(own_keys[0], (W, F, NX, NY, NZ), 1.0, 6.0, ((2, 8), (3, 2)))
    gm_index = draw_gm_index(jax.random.fold_in(seeds[3], 71), part)
    partners = draw_partners(jax.random.fold_in(seeds[3], 71), part)
    return dict(bold=bold, gm_index=gm_index, partners=partners)


side_weight = math.exp(-0.5) / (1.0 + 2.0 * math.exp(-0.5))
centre_weight = 1.0 / (1.0 + 2.0 * math.exp(-0.5))

def gaussian_blur(padded):
    first = side_weight * padded[:, :, :-2] + centre_weight * padded[:, :, 1:-1] + side_weight * padded[:, :, 2:]
    second = side_weight * first[:, :, :, :-2] + centre_weight * first[:, :, :, 1:-1] + side_weight * first[:, :, :, 2:]
    return side_weight * second[..., :-2] + centre_weight * second[..., 1:-1] + side_weight * second[..., 2:]

def standardize(smooth):
    windows, frames = (smooth.shape[0], smooth.shape[1])
    series = smooth.reshape(windows, frames, -1)
    centred = series - lax.optimization_barrier(jnp.mean(series, axis=1, keepdims=True))
    spread = lax.optimization_barrier(jnp.mean(centred * centred, axis=1, keepdims=True))
    scored = centred * lax.rsqrt((spread + 1e-05) * frames)
    return jnp.transpose(scored, (2, 0, 1)).astype(jnp.bfloat16)

def reference(bold, gm_index, partners):
    padded = jnp.pad(bold.astype(jnp.float32), ((0, 0), (0, 0), (1, 1), (1, 1), (1, 1)))
    scored = standardize(gaussian_blur(padded))
    row_ids = jnp.arange(NB * BLOCK).astype(jnp.int32)
    slab = row_ids // ROWS_DEV
    slab_row = slab // N_COL
    slab_col = slab % N_COL
    voxel = jnp.maximum(gm_index, 0).astype(jnp.int32)
    local_x = voxel // (SY * SZ)
    local_y = voxel // SZ % SY
    local_z = voxel % SZ
    global_ids = ((slab_row * SX + local_x) * NY + slab_col * SY + local_y) * NZ + local_z
    picked = jnp.take(scored, global_ids.astype(jnp.int32), axis=0)
    panel = jnp.where((gm_index >= 0)[:, None, None], picked, jnp.zeros_like(picked))
    blocks = panel.reshape(NB, BLOCK, W, F)

    def block_tiles(inputs):
        local_block, partner_ids = inputs
        partner_rows = jnp.take(blocks, jnp.maximum(partner_ids, 0).astype(jnp.int32), axis=0)
        tiles_out = jnp.einsum('awf,kbwf->kwab', local_block.astype(jnp.float32), partner_rows.astype(jnp.float32))
        tiles_out = jnp.where((partner_ids >= 0)[:, None, None, None], tiles_out, jnp.zeros_like(tiles_out))
        return tiles_out.astype(jnp.bfloat16)
    return lax.map(block_tiles, (blocks, partners))
```

```python
import functools
import math

import jax
import jax.numpy as jnp
from jax import lax
from jax.experimental import pallas as pl
from jax.experimental.pallas import tpu as pltpu
from jax.sharding import PartitionSpec as P

HOP = 2
MESH = pl.DeviceIdType.MESH
CHUNKS = 4
DETOUR = 0

side_weight = math.exp(-0.5) / (1.0 + 2.0 * math.exp(-0.5))
centre_weight = 1.0 / (1.0 + 2.0 * math.exp(-0.5))
SPAN, SPAN_SIDE, SPAN_CENTRE = 135.0, 37.0, 61.0


def three(low, mid, high):
    return side_weight * (low + high) + centre_weight * mid


def panel_kernel(
    rows,
    gm_ref,
    bold_ref,
    cand_ref,
    scale_ref,
    bold,
    ext,
    mean_own,
    mean_ext,
    mean_x,
    mean_face,
    mean_xy,
    gm_pair,
    pick,
    xf,
    face_out,
    face_in,
    lhs,
    square,
    panel,
    scale,
    local_sem,
    raw_send,
    raw_recv,
    face_send,
    face_recv,
    small_send,
    small_recv,
    own_sem,
    panel_send,
    panel_recv,
    across_send,
    across_recv,
):
    windows, frames, sx, sy, sz = bold_ref.shape
    count = gm_ref.shape[1]
    blocks = panel.shape[1]
    chunks = face_in.shape[0]
    n = frames // chunks
    r = lax.axis_index("row")
    c = lax.axis_index("col")
    a = lax.rem(r, 2)
    ahead = 1 - 2 * a
    pair = r + ahead
    fwd = lax.rem(r + 2 * ahead + rows, rows)
    back = lax.rem(r - 2 * ahead + rows, rows)
    diag = lax.rem(r - ahead + rows, rows)
    other = {"col": 1 - c}
    to_pair, to_fwd, to_back, to_diag = {"row": pair}, {"row": fwd}, {"row": back}, {"row": diag}
    level = r + (rows - 2 * r - 1) * a
    has_fwd = level < rows - 2
    has_back = level > 0
    mine = 1 + 2 * a
    theirs = 3 - 2 * a
    back_edge = 5 * a
    fwd_edge = 5 - 5 * a

    barrier = pltpu.get_barrier_semaphore()
    for target in (to_pair, to_fwd, to_back, to_diag, other):
        pl.semaphore_signal(barrier, inc=1, device_id=target, device_id_type=MESH)

    def load(w):
        return pltpu.make_async_copy(bold_ref.at[w], bold.at[w], local_sem.at[w])

    def load_own(x):
        return pltpu.make_async_copy(bold_ref.at[a, :, x], ext.at[mine + x], local_sem.at[2 + x])

    for w in range(windows):
        load(w).start()
    for x in range(sx):
        load_own(x).start()

    def remote(src, dst, send_sem, recv_sem, target):
        return pltpu.make_async_remote_copy(
            src_ref=src,
            dst_ref=dst,
            send_sem=send_sem,
            recv_sem=recv_sem,
            device_id=target,
            device_id_type=MESH,
        )

    def at(k):
        return pl.ds(pl.multiple_of(k * n, n), n)

    def raw_outer(k):
        return remote(
            bold_ref.at[1 - a, at(k), a], ext.at[mine + a, at(k)],
            raw_send.at[k, 0], raw_recv.at[k, 0], to_pair,
        )

    def raw_inner(k):
        return remote(
            bold_ref.at[1 - a, at(k), 1 - a], ext.at[mine + 1 - a, at(k)],
            raw_send.at[k, 1], raw_recv.at[k, 1], to_pair,
        )

    def raw_back(k):
        return remote(
            bold_ref.at[a, at(k), a], ext.at[fwd_edge, at(k)],
            raw_send.at[k, 2], raw_recv.at[k, 2], to_back,
        )

    def raw_fwd(k):
        return remote(
            ext.at[theirs + 1 - a, at(k)], ext.at[back_edge, at(k)],
            raw_send.at[k, 3], raw_recv.at[k, 3], to_fwd,
        )

    def gm_copy():
        return remote(gm_ref, gm_pair, small_send.at[0], small_recv.at[0], to_pair)

    def mean_pair():
        return remote(
            mean_own.at[1 - a], mean_ext.at[pl.ds(mine, sx)], small_send.at[1], small_recv.at[1], to_pair
        )

    def mean_back():
        return remote(
            mean_own.at[a, a], mean_ext.at[fwd_edge], small_send.at[2], small_recv.at[2], to_back
        )

    def mean_diag():
        return remote(
            mean_own.at[1 - a, a], mean_ext.at[fwd_edge], small_send.at[3], small_recv.at[3], to_diag
        )

    def mean_other():
        return remote(mean_x, mean_face, small_send.at[4], small_recv.at[4], other)

    def face(k):
        return remote(face_out.at[k], face_in.at[k], face_send.at[k], face_recv.at[k], other)

    def build(gm, p):
        tile = lax.shift_right_arithmetic(gm, 7)
        lane = jnp.bitwise_and(gm, sz - 1)
        z = lax.broadcasted_iota(jnp.int32, (sz, count), 0)

        def fill(step, carry):
            start = pl.multiple_of(step * sz, sz)
            away = jnp.abs(z - jnp.where(tile == step, lane, 4 * sz))
            weight = jnp.where(away == 0, SPAN_CENTRE, jnp.where(away == 1, SPAN_SIDE, 0.0))
            pick[p, pl.ds(start, sz), :] = weight.astype(jnp.bfloat16)
            return carry

        lax.fori_loop(0, sx * sy, fill, 0)

    @pl.when(jnp.logical_not(has_back))
    def _():
        ext[back_edge] = jnp.zeros(ext.shape[1:], ext.dtype)
        mean_ext[back_edge] = jnp.zeros(mean_ext.shape[1:], mean_ext.dtype)

    @pl.when(jnp.logical_not(has_fwd))
    def _():
        ext[fwd_edge] = jnp.zeros(ext.shape[1:], ext.dtype)
        mean_ext[fwd_edge] = jnp.zeros(mean_ext.shape[1:], mean_ext.dtype)

    pl.semaphore_wait(barrier, 5)

    gm_copy().start()
    for k in range(chunks):
        raw_outer(k).start()
        raw_inner(k).start()

        @pl.when(has_back)
        def _():
            raw_back(k).start()

    for w in range(windows):
        load(w).wait()
    part = 16

    def add_frames(step, total):
        here = bold[:, pl.ds(step * part, part)].astype(jnp.float32)
        return total + jnp.sum(here, axis=1)

    total = lax.fori_loop(
        0, frames // part, add_frames, jnp.zeros((windows, sx, sy, sz), jnp.float32)
    )
    mean_own[...] = total * (1.0 / frames)
    mean_pair().start()

    @pl.when(has_back)
    def _():
        mean_back().start()
        mean_diag().start()

    mean_ext[pl.ds(mine, sx)] = mean_own[a]

    build(gm_ref[...], a)

    def relay_raw(k):
        raw_outer(k).wait_recv()

        @pl.when(has_fwd)
        def _():
            raw_fwd(k).start()

    relay_raw(0)
    gm_copy().wait_recv()
    build(gm_pair[...], 1 - a)

    mean_pair().wait_recv()

    @pl.when(has_fwd)
    def _():
        mean_back().wait_recv()

    @pl.when(has_back)
    def _():
        remote(
            mean_own.at[1 - a, a], mean_ext.at[back_edge], small_send.at[3], small_recv.at[3], to_diag
        ).wait_recv()

    for l in range(2 * sx):
        mean_x[l] = three(mean_ext[l], mean_ext[l + 1], mean_ext[l + 2])
    mean_other().start()
    mean_other().wait_recv()
    nothing = jnp.zeros((1, sz), jnp.float32)
    for l in range(2 * sx):
        inner = mean_x[l]
        first = jnp.where(c == 1, mean_face[l, sy - 1 : sy, :], nothing)
        last = jnp.where(c == 0, mean_face[l, 0:1, :], nothing)
        low = jnp.concatenate([first, inner[: sy - 1]], axis=0)
        high = jnp.concatenate([inner[1:], last], axis=0)
        mean_xy[l] = three(low, inner, high)
    square[...] = jnp.zeros_like(square)
    for x in range(sx):
        load_own(x).wait()

    def slot(offset, col):
        return (offset + HOP) * 2 + col

    def made(k, p):
        if isinstance(k, int) and k == chunks:
            return scale.at[p]
        return panel.at[p, :, at(k), :]

    def place(k, offset, w):
        if isinstance(k, int) and k == chunks:
            return scale_ref.at[slot(offset, c), w]
        return cand_ref.at[slot(offset, c), w, :, at(k), :]

    def piece(k, src, offset, w, which, target):
        return remote(
            src, place(k, offset, w),
            panel_send.at[k, which], panel_recv.at[k, offset + HOP, w], target,
        )

    def y_other(k):
        return piece(k, made(k, 1 - a), 0 * a, a, 0, to_pair)

    def y_self(k):
        return piece(k, made(k, a), -ahead, a, 1, to_pair)

    def fwd_self(k):
        return piece(k, made(k, a), -2 * ahead, a, 2, to_fwd)

    def fwd_other(k):
        return piece(k, made(k, 1 - a), -ahead, a, 3, to_fwd)

    def back_self(k):
        return piece(k, made(k, a), 2 * ahead, a, 4, to_back)

    def fwd_relay(k):
        return piece(k, place(k, 0 * a, 1 - a), -2 * ahead, 1 - a, 5, to_fwd)

    def y_relay_back(k):
        return piece(k, place(k, -ahead, a), -2 * ahead, a, 6, to_pair)

    def y_relay_fwd(k):
        return piece(k, place(k, 2 * ahead, a), ahead, a, 7, to_pair)

    def fwd_detour(k):
        return piece(k, place(k, ahead, 1 - a), -ahead, 1 - a, 6, to_fwd)

    def back_detour(k):
        return piece(k, place(k, 0 * a, 1 - a), 2 * ahead, 1 - a, 7, to_back)

    def arrived(k, offset, w):
        remote(
            place(k, offset, w), place(k, offset, w),
            panel_send.at[k, 0], panel_recv.at[k, offset + HOP, w], to_pair,
        ).wait_recv()

    def across(k, src, offset, w):
        return remote(
            src, place(k, offset, w),
            across_send.at[k, offset + HOP, w], across_recv.at[k, offset + HOP, w], other,
        )

    def across_own(k, p):
        return across(k, made(k, p), p - a, a)

    def across_in(k, offset, w):
        return across(k, place(k, offset, w), offset, w)

    def own(k, p):
        return pltpu.make_async_copy(made(k, p), place(k, p - a, a), own_sem.at[k, p])

    def emit(k):
        fwd_self(k).start()
        y_other(k).start()
        back_self(k).start()
        y_self(k).start()
        fwd_other(k).start()
        for p in range(2):
            own(k, p).start()
            across_own(k, p).start()

    step_frames = 8

    def compute(k, carry):

        @pl.when(k + 1 < chunks)
        def _():
            relay_raw(k + 1)

        raw_inner(k).wait_recv()

        @pl.when(has_fwd)
        def _():
            raw_back(k).wait_recv()

        @pl.when(has_back)
        def _():
            raw_fwd(k).wait_recv()

        def filter_x(step, inner):
            here = pl.ds(k * n + step * step_frames, step_frames)
            flat = pl.ds(pl.multiple_of(step * step_frames * sy, step_frames * sy), step_frames * sy)
            layer = [ext[l, here].astype(jnp.float32) for l in range(2 * sx + 2)]
            for l in range(2 * sx):
                xf[l, flat, :] = three(layer[l], layer[l + 1], layer[l + 2]).reshape(step_frames * sy, sz)
            return inner

        lax.fori_loop(0, n // step_frames, filter_x, 0)

        edge = (sy - 1) * (1 - c)
        for l in range(2 * sx):
            face_out[k, l] = xf[l, pl.ds(edge, n, stride=sy), :]
        face(k).start()

        def row_of(l, y):
            return xf[l, pl.ds(y, n, stride=sy), :]

        def finish(l, y, low, mid, high):
            value = three(low, mid, high) - mean_xy[l, y : y + 1, :]
            start = ((l % sx) * sy + y) * sz
            lhs[l // sx, :, start : start + sz] = value.astype(jnp.bfloat16)

        for l in range(2 * sx):
            low, mid = row_of(l, 0), row_of(l, 1)
            for y in range(1, sy - 1):
                high = row_of(l, y + 1)
                finish(l, y, low, mid, high)
                low, mid = mid, high
        face(k).wait_recv()
        for l in range(2 * sx):
            outside = face_in[k, l]
            finish(l, 0, jnp.where(c == 1, outside, 0.0), row_of(l, 0), row_of(l, 1))
            finish(l, sy - 1, row_of(l, sy - 2), row_of(l, sy - 1), jnp.where(c == 0, outside, 0.0))

        wide = 2 * sz
        for p in range(2):
            for j in range(count // wide):
                cols = slice(j * wide, (j + 1) * wide)
                got = jnp.dot(lhs[p], pick[p, :, cols], preferred_element_type=jnp.float32)
                square[p, :, cols] += jnp.sum(got * got, axis=0, keepdims=True)
                small = got.astype(jnp.bfloat16)
                panel[p, 2 * j, at(k), :] = small[:, :sz]
                panel[p, 2 * j + 1, at(k), :] = small[:, sz:]
        emit(k)
        return carry

    lax.fori_loop(0, chunks, compute, 0)

    for p in range(2):
        value = lax.rsqrt(square[p] + 1e-05 * frames * SPAN * SPAN)
        for b in range(blocks):
            scale[p, b : b + 1, :] = value[:, b * sz : (b + 1) * sz]
    emit(chunks)

    def from_pair(k):
        arrived(k, 0 * a, 1 - a)
        fwd_relay(k).start()
        if k == DETOUR:
            back_detour(k).start()
        across_in(k, 0 * a, 1 - a).start()
        arrived(k, ahead, 1 - a)
        if k == DETOUR:
            fwd_detour(k).start()
        across_in(k, ahead, 1 - a).start()

    def from_level(k):
        arrived(k, -ahead, a)
        if k != DETOUR:
            y_relay_back(k).start()
        across_in(k, -ahead, a).start()
        arrived(k, 2 * ahead, a)
        if k != DETOUR:
            y_relay_fwd(k).start()
        across_in(k, 2 * ahead, a).start()
        arrived(k, -2 * ahead, a)
        across_in(k, -2 * ahead, a).start()

    def from_relays(k):
        for offset in (-2 * ahead, -ahead, 2 * ahead):
            arrived(k, offset, 1 - a)
            across_in(k, offset, 1 - a).start()

    everything = [*range(chunks), chunks]
    from_pair(0)
    from_level(0)
    for k in range(1, chunks - 1):
        from_pair(k)
        from_level(k)
    from_pair(chunks - 1)
    from_pair(chunks)
    from_level(chunks)
    from_level(chunks - 1)
    for k in everything:
        from_relays(k)

    for k in everything:
        for offset in range(-HOP, HOP + 1):
            for w in range(windows):
                across(k, place(k, offset, w), offset, w).wait_recv()

    gm_copy().wait_send()
    mean_pair().wait_send()
    mean_other().wait_send()

    @pl.when(has_back)
    def _():
        mean_back().wait_send()
        mean_diag().wait_send()

    for k in range(chunks):
        raw_outer(k).wait_send()
        raw_inner(k).wait_send()
        face(k).wait_send()

        @pl.when(has_back)
        def _():
            raw_back(k).wait_send()

        @pl.when(has_fwd)
        def _():
            raw_fwd(k).wait_send()

    for k in everything:
        for send in (y_other, y_self, fwd_self, fwd_other, back_self, fwd_relay):
            send(k).wait_send()
        for send in (fwd_detour, back_detour) if k == DETOUR else (y_relay_back, y_relay_fwd):
            send(k).wait_send()
        for p in range(2):
            own(k, p).wait()
        for offset in range(-HOP, HOP + 1):
            for w in range(windows):
                across(k, place(k, offset, w), offset, w).wait_send()


def tile_kernel(rows, cols, partners_ref, cand_ref, scale_ref, out_ref):
    i = pl.program_id(0)
    blocks = cand_ref.shape[2]
    block_rows = cand_ref.shape[4]
    windows = cand_ref.shape[1]
    slots = out_ref.shape[1]
    r = lax.axis_index("row")
    c = lax.axis_index("col")
    home = HOP * cols + c
    local = [cand_ref[home, w, i].T for w in range(windows)]
    left = [
        jnp.broadcast_to(scale_ref[home, w, pl.ds(i, 1), :], (block_rows, block_rows)).T
        for w in range(windows)
    ]
    for k in range(0, slots, 2):
        found = []
        for q in (k, k + 1):
            name = partners_ref[i, q]
            safe = jnp.maximum(name, 0)
            slab = safe // blocks
            distance = lax.rem(slab // cols - r + HOP + rows, rows)
            place = jnp.where(name >= 0, distance * cols + lax.rem(slab, cols), 0)
            found.append((name >= 0, place, lax.rem(safe, blocks)))
        for w in range(windows):
            right = jnp.concatenate([cand_ref[s, w, b] for _, s, b in found], axis=1)
            tiles = jnp.dot(local[w], right, preferred_element_type=jnp.float32)
            for n, (present, s, b) in enumerate(found):
                tile = tiles[:, n * block_rows : (n + 1) * block_rows]
                factor = jnp.where(present, scale_ref[s, w, pl.ds(b, 1), :], 0.0)
                out_ref[0, k + n, w] = (tile * left[w] * factor).astype(out_ref.dtype)


def on_device(rows, cols, bold, gm_index, partners):
    windows, frames, sx, sy, sz = bold.shape
    voxels = sx * sy * sz
    count = gm_index.shape[0]
    blocks, slots = partners.shape
    block_rows = count // blocks
    slabs = (2 * HOP + 1) * cols
    bf16, f32 = jnp.bfloat16, jnp.float32
    n = frames // CHUNKS
    dma = pltpu.SemaphoreType.DMA
    cand, scale = pl.pallas_call(
        functools.partial(panel_kernel, rows),
        out_shape=(
            jax.ShapeDtypeStruct((slabs, windows, blocks, frames, block_rows), bf16),
            jax.ShapeDtypeStruct((slabs, windows, blocks, block_rows), f32),
        ),
        in_specs=[pl.BlockSpec(memory_space=pltpu.VMEM), pl.BlockSpec(memory_space=pltpu.HBM)],
        out_specs=(pl.BlockSpec(memory_space=pl.ANY), pl.BlockSpec(memory_space=pl.ANY)),
        scratch_shapes=[
            pltpu.VMEM((windows, frames, sx, sy, sz), bf16),
            pltpu.VMEM((2 * sx + 2, frames, sy, sz), bf16),
            pltpu.VMEM((windows, sx, sy, sz), f32),
            pltpu.VMEM((2 * sx + 2, sy, sz), f32),
            pltpu.VMEM((2 * sx, sy, sz), f32),
            pltpu.VMEM((2 * sx, sy, sz), f32),
            pltpu.VMEM((2 * sx, sy, sz), f32),
            pltpu.VMEM((1, count), jnp.int32),
            pltpu.VMEM((2, voxels, count), bf16),
            pltpu.VMEM((2 * sx, n * sy, sz), f32),
            pltpu.VMEM((CHUNKS, 2 * sx, n, sz), f32),
            pltpu.VMEM((CHUNKS, 2 * sx, n, sz), f32),
            pltpu.VMEM((2, n, voxels), bf16),
            pltpu.VMEM((2, 1, count), f32),
            pltpu.VMEM((2, blocks, frames, block_rows), bf16),
            pltpu.VMEM((2, blocks, block_rows), f32),
            dma((4,)),
            dma((CHUNKS, 4)),
            dma((CHUNKS, 4)),
            dma((CHUNKS,)),
            dma((CHUNKS,)),
            dma((5,)),
            dma((5,)),
            dma((CHUNKS + 1, 2)),
            dma((CHUNKS + 1, 8)),
            dma((CHUNKS + 1, 2 * HOP + 1, 2)),
            dma((CHUNKS + 1, 2 * HOP + 1, 2)),
            dma((CHUNKS + 1, 2 * HOP + 1, 2)),
        ],
        compiler_params=pltpu.CompilerParams(
            collective_id=0, has_side_effects=True, vmem_limit_bytes=40 * 1024 * 1024
        ),
        name="panels",
    )(gm_index.reshape(1, count), bold)
    return pl.pallas_call(
        functools.partial(tile_kernel, rows, cols),
        out_shape=jax.ShapeDtypeStruct((blocks, slots, windows, block_rows, block_rows), bf16),
        grid_spec=pltpu.PrefetchScalarGridSpec(
            num_scalar_prefetch=1,
            grid=(blocks,),
            in_specs=[pl.BlockSpec(memory_space=pltpu.VMEM)] * 2,
            out_specs=pl.BlockSpec(
                (1, slots, windows, block_rows, block_rows), lambda i, names: (i, 0, 0, 0, 0)
            ),
        ),
        compiler_params=pltpu.CompilerParams(vmem_limit_bytes=40 * 1024 * 1024),
        name="tiles",
    )(partners, cand, scale)


def solution(mesh):
    rows, cols = mesh.shape["row"], mesh.shape["col"]
    in_specs = (P("subj", None, "row", "col", None), P(("row", "col")), P(("row", "col"), None))
    out_specs = P(("row", "col"), None, "subj", None, None)
    return jax.shard_map(
        functools.partial(on_device, rows, cols),
        mesh=mesh,
        in_specs=in_specs,
        out_specs=out_specs,
        check_vma=False,
    )
```

```python
import functools
import math

import jax
import jax.numpy as jnp
from jax import lax
from jax.experimental import pallas as pl
from jax.experimental.pallas import tpu as pltpu
from jax.sharding import PartitionSpec as P

HOP = 2
MESH = pl.DeviceIdType.MESH
CHUNKS = 4
DETOUR = 0

side_weight = math.exp(-0.5) / (1.0 + 2.0 * math.exp(-0.5))
centre_weight = 1.0 / (1.0 + 2.0 * math.exp(-0.5))
SPAN, SPAN_SIDE, SPAN_CENTRE = 135.0, 37.0, 61.0


def three(low, mid, high):
    return side_weight * (low + high) + centre_weight * mid


def panel_kernel(
    rows,
    gm_ref,
    bold_ref,
    cand_ref,
    scale_ref,
    bold,
    ext,
    mean_own,
    mean_ext,
    mean_x,
    mean_face,
    mean_xy,
    gm_pair,
    pick,
    xf,
    face_out,
    face_in,
    lhs,
    square,
    panel,
    scale,
    local_sem,
    raw_send,
    raw_recv,
    face_send,
    face_recv,
    small_send,
    small_recv,
    own_sem,
    panel_send,
    panel_recv,
    across_send,
    across_recv,
):
    windows, frames, sx, sy, sz = bold_ref.shape
    count = gm_ref.shape[1]
    blocks = panel.shape[1]
    chunks = face_in.shape[0]
    n = frames // chunks
    r = lax.axis_index("row")
    c = lax.axis_index("col")
    a = lax.rem(r, 2)
    ahead = 1 - 2 * a
    pair = r + ahead
    fwd = lax.rem(r + 2 * ahead + rows, rows)
    back = lax.rem(r - 2 * ahead + rows, rows)
    diag = lax.rem(r - ahead + rows, rows)
    other = {"col": 1 - c}
    to_pair, to_fwd, to_back, to_diag = {"row": pair}, {"row": fwd}, {"row": back}, {"row": diag}
    level = r + (rows - 2 * r - 1) * a
    has_fwd = level < rows - 2
    has_back = level > 0
    mine = 1 + 2 * a
    theirs = 3 - 2 * a
    back_edge = 5 * a
    fwd_edge = 5 - 5 * a

    barrier = pltpu.get_barrier_semaphore()
    for target in (to_pair, to_fwd, to_back, to_diag, other):
        pl.semaphore_signal(barrier, inc=1, device_id=target, device_id_type=MESH)

    def load(w):
        return pltpu.make_async_copy(bold_ref.at[w], bold.at[w], local_sem.at[w])

    def load_own(x):
        return pltpu.make_async_copy(bold_ref.at[a, :, x], ext.at[mine + x], local_sem.at[2 + x])

    for w in range(windows):
        load(w).start()
    for x in range(sx):
        load_own(x).start()

    def remote(src, dst, send_sem, recv_sem, target):
        return pltpu.make_async_remote_copy(
            src_ref=src,
            dst_ref=dst,
            send_sem=send_sem,
            recv_sem=recv_sem,
            device_id=target,
            device_id_type=MESH,
        )

    def at(k):
        return pl.ds(pl.multiple_of(k * n, n), n)

    def raw_outer(k):
        return remote(
            bold_ref.at[1 - a, at(k), a], ext.at[mine + a, at(k)],
            raw_send.at[k, 0], raw_recv.at[k, 0], to_pair,
        )

    def raw_inner(k):
        return remote(
            bold_ref.at[1 - a, at(k), 1 - a], ext.at[mine + 1 - a, at(k)],
            raw_send.at[k, 1], raw_recv.at[k, 1], to_pair,
        )

    def raw_back(k):
        return remote(
            bold_ref.at[a, at(k), a], ext.at[fwd_edge, at(k)],
            raw_send.at[k, 2], raw_recv.at[k, 2], to_back,
        )

    def raw_fwd(k):
        return remote(
            ext.at[theirs + 1 - a, at(k)], ext.at[back_edge, at(k)],
            raw_send.at[k, 3], raw_recv.at[k, 3], to_fwd,
        )

    def gm_copy():
        return remote(gm_ref, gm_pair, small_send.at[0], small_recv.at[0], to_pair)

    def mean_pair():
        return remote(
            mean_own.at[1 - a], mean_ext.at[pl.ds(mine, sx)], small_send.at[1], small_recv.at[1], to_pair
        )

    def mean_back():
        return remote(
            mean_own.at[a, a], mean_ext.at[fwd_edge], small_send.at[2], small_recv.at[2], to_back
        )

    def mean_diag():
        return remote(
            mean_own.at[1 - a, a], mean_ext.at[fwd_edge], small_send.at[3], small_recv.at[3], to_diag
        )

    def mean_other():
        return remote(mean_x, mean_face, small_send.at[4], small_recv.at[4], other)

    def face(k):
        return remote(face_out.at[k], face_in.at[k], face_send.at[k], face_recv.at[k], other)

    def build(gm, p):
        tile = lax.shift_right_arithmetic(gm, 7)
        lane = jnp.bitwise_and(gm, sz - 1)
        z = lax.broadcasted_iota(jnp.int32, (sz, count), 0)

        def fill(step, carry):
            start = pl.multiple_of(step * sz, sz)
            away = jnp.abs(z - jnp.where(tile == step, lane, 4 * sz))
            weight = jnp.where(away == 0, SPAN_CENTRE, jnp.where(away == 1, SPAN_SIDE, 0.0))
            pick[p, pl.ds(start, sz), :] = weight.astype(jnp.bfloat16)
            return carry

        lax.fori_loop(0, sx * sy, fill, 0)

    @pl.when(jnp.logical_not(has_back))
    def _():
        ext[back_edge] = jnp.zeros(ext.shape[1:], ext.dtype)
        mean_ext[back_edge] = jnp.zeros(mean_ext.shape[1:], mean_ext.dtype)

    @pl.when(jnp.logical_not(has_fwd))
    def _():
        ext[fwd_edge] = jnp.zeros(ext.shape[1:], ext.dtype)
        mean_ext[fwd_edge] = jnp.zeros(mean_ext.shape[1:], mean_ext.dtype)

    pl.semaphore_wait(barrier, 5)

    gm_copy().start()
    raw_outer(0).start()
    raw_inner(0).start()

    @pl.when(has_back)
    def _():
        raw_back(0).start()

    for w in range(windows):
        load(w).wait()
    part = 16

    def add_frames(step, total):
        here = bold[:, pl.ds(step * part, part)].astype(jnp.float32)
        return total + jnp.sum(here, axis=1)

    total = lax.fori_loop(
        0, frames // part, add_frames, jnp.zeros((windows, sx, sy, sz), jnp.float32)
    )
    mean_own[...] = total * (1.0 / frames)
    mean_pair().start()

    @pl.when(has_back)
    def _():
        mean_back().start()
        mean_diag().start()

    for k in range(1, chunks):
        raw_outer(k).start()
    for k in range(1, chunks):
        raw_inner(k).start()
    for k in range(1, chunks):

        @pl.when(has_back)
        def _():
            raw_back(k).start()

    mean_ext[pl.ds(mine, sx)] = mean_own[a]

    build(gm_ref[...], a)

    def relay_raw(k):
        raw_outer(k).wait_recv()

        @pl.when(has_fwd)
        def _():
            raw_fwd(k).start()

    relay_raw(0)
    gm_copy().wait_recv()
    build(gm_pair[...], 1 - a)

    mean_pair().wait_recv()

    @pl.when(has_fwd)
    def _():
        mean_back().wait_recv()

    @pl.when(has_back)
    def _():
        remote(
            mean_own.at[1 - a, a], mean_ext.at[back_edge], small_send.at[3], small_recv.at[3], to_diag
        ).wait_recv()

    for l in range(2 * sx):
        mean_x[l] = three(mean_ext[l], mean_ext[l + 1], mean_ext[l + 2])
    mean_other().start()
    mean_other().wait_recv()
    nothing = jnp.zeros((1, sz), jnp.float32)
    for l in range(2 * sx):
        inner = mean_x[l]
        first = jnp.where(c == 1, mean_face[l, sy - 1 : sy, :], nothing)
        last = jnp.where(c == 0, mean_face[l, 0:1, :], nothing)
        low = jnp.concatenate([first, inner[: sy - 1]], axis=0)
        high = jnp.concatenate([inner[1:], last], axis=0)
        mean_xy[l] = three(low, inner, high)
    square[...] = jnp.zeros_like(square)
    for x in range(sx):
        load_own(x).wait()

    def slot(offset, col):
        return (offset + HOP) * 2 + col

    def made(k, p):
        if isinstance(k, int) and k == chunks:
            return scale.at[p]
        return panel.at[p, :, at(k), :]

    def place(k, offset, w):
        if isinstance(k, int) and k == chunks:
            return scale_ref.at[slot(offset, c), w]
        return cand_ref.at[slot(offset, c), w, :, at(k), :]

    def piece(k, src, offset, w, which, target):
        return remote(
            src, place(k, offset, w),
            panel_send.at[k, which], panel_recv.at[k, offset + HOP, w], target,
        )

    def y_other(k):
        return piece(k, made(k, 1 - a), 0 * a, a, 0, to_pair)

    def y_self(k):
        return piece(k, made(k, a), -ahead, a, 1, to_pair)

    def fwd_self(k):
        return piece(k, made(k, a), -2 * ahead, a, 2, to_fwd)

    def fwd_other(k):
        return piece(k, made(k, 1 - a), -ahead, a, 3, to_fwd)

    def back_self(k):
        return piece(k, made(k, a), 2 * ahead, a, 4, to_back)

    def fwd_relay(k):
        return piece(k, place(k, 0 * a, 1 - a), -2 * ahead, 1 - a, 5, to_fwd)

    def y_relay_back(k):
        return piece(k, place(k, -ahead, a), -2 * ahead, a, 6, to_pair)

    def y_relay_fwd(k):
        return piece(k, place(k, 2 * ahead, a), ahead, a, 7, to_pair)

    def fwd_detour(k):
        return piece(k, place(k, ahead, 1 - a), -ahead, 1 - a, 8, to_fwd)

    def back_detour(k):
        return piece(k, place(k, 0 * a, 1 - a), 2 * ahead, 1 - a, 9, to_back)

    def arrived(k, offset, w):
        remote(
            place(k, offset, w), place(k, offset, w),
            panel_send.at[k, 0], panel_recv.at[k, offset + HOP, w], to_pair,
        ).wait_recv()

    def across(k, src, offset, w):
        return remote(
            src, place(k, offset, w),
            across_send.at[k, offset + HOP, w], across_recv.at[k, offset + HOP, w], other,
        )

    def across_own(k, p):
        return across(k, made(k, p), p - a, a)

    def across_in(k, offset, w):
        return across(k, place(k, offset, w), offset, w)

    def own(k, p):
        return pltpu.make_async_copy(made(k, p), place(k, p - a, a), own_sem.at[k, p])

    def emit(k):
        fwd_self(k).start()
        y_other(k).start()
        back_self(k).start()
        y_self(k).start()
        fwd_other(k).start()
        for p in range(2):
            own(k, p).start()
            across_own(k, p).start()

    step_frames = 8

    def compute(k, carry):

        raw_inner(k).wait_recv()

        @pl.when(has_fwd)
        def _():
            raw_back(k).wait_recv()

        @pl.when(has_back)
        def _():
            raw_fwd(k).wait_recv()

        def filter_x(step, inner):
            here = pl.ds(k * n + step * step_frames, step_frames)
            flat = pl.ds(pl.multiple_of(step * step_frames * sy, step_frames * sy), step_frames * sy)
            layer = [ext[l, here].astype(jnp.float32) for l in range(2 * sx + 2)]
            for l in range(2 * sx):
                xf[l, flat, :] = three(layer[l], layer[l + 1], layer[l + 2]).reshape(step_frames * sy, sz)
            return inner

        lax.fori_loop(0, n // step_frames, filter_x, 0)

        edge = (sy - 1) * (1 - c)
        for l in range(2 * sx):
            face_out[k, l] = xf[l, pl.ds(edge, n, stride=sy), :]
        face(k).start()

        @pl.when(k == 0)
        def _():
            relay_raw(1)

        def row_of(l, y):
            return xf[l, pl.ds(y, n, stride=sy), :]

        def finish(l, y, low, mid, high):
            value = three(low, mid, high) - mean_xy[l, y : y + 1, :]
            start = ((l % sx) * sy + y) * sz
            lhs[l // sx, :, start : start + sz] = value.astype(jnp.bfloat16)

        for l in range(2 * sx):
            low, mid = row_of(l, 0), row_of(l, 1)
            for y in range(1, sy - 1):
                high = row_of(l, y + 1)
                finish(l, y, low, mid, high)
                low, mid = mid, high
        face(k).wait_recv()
        for l in range(2 * sx):
            outside = face_in[k, l]
            finish(l, 0, jnp.where(c == 1, outside, 0.0), row_of(l, 0), row_of(l, 1))
            finish(l, sy - 1, row_of(l, sy - 2), row_of(l, sy - 1), jnp.where(c == 0, outside, 0.0))

        wide = 2 * sz
        for p in range(2):
            for j in range(count // wide):
                cols = slice(j * wide, (j + 1) * wide)
                got = jnp.dot(lhs[p], pick[p, :, cols], preferred_element_type=jnp.float32)
                square[p, :, cols] += jnp.sum(got * got, axis=0, keepdims=True)
                small = got.astype(jnp.bfloat16)
                panel[p, 2 * j, at(k), :] = small[:, :sz]
                panel[p, 2 * j + 1, at(k), :] = small[:, sz:]
        emit(k)

        @pl.when(k == 0)
        def _():
            for later in range(2, chunks):
                relay_raw(later)

        return carry

    lax.fori_loop(0, chunks, compute, 0)

    for p in range(2):
        value = lax.rsqrt(square[p] + 1e-05 * frames * SPAN * SPAN)
        for b in range(blocks):
            scale[p, b : b + 1, :] = value[:, b * sz : (b + 1) * sz]
    emit(chunks)

    def relays_back(k):
        return jnp.logical_not(has_back) if k == DETOUR else r >= 0

    def relays_fwd(k):
        return jnp.logical_not(has_fwd) if k == DETOUR else r >= 0

    def from_pair(k):
        arrived(k, 0 * a, 1 - a)
        fwd_relay(k).start()
        if k == DETOUR:

            @pl.when(has_back)
            def _():
                back_detour(k).start()

        across_in(k, 0 * a, 1 - a).start()
        arrived(k, ahead, 1 - a)
        if k == DETOUR:

            @pl.when(has_fwd)
            def _():
                fwd_detour(k).start()

        across_in(k, ahead, 1 - a).start()

    def from_level(k):
        arrived(k, -ahead, a)

        @pl.when(relays_back(k))
        def _():
            y_relay_back(k).start()

        across_in(k, -ahead, a).start()
        arrived(k, 2 * ahead, a)

        @pl.when(relays_fwd(k))
        def _():
            y_relay_fwd(k).start()

        across_in(k, 2 * ahead, a).start()
        arrived(k, -2 * ahead, a)
        across_in(k, -2 * ahead, a).start()

    def from_relays(k):
        for offset in (-2 * ahead, -ahead, 2 * ahead):
            arrived(k, offset, 1 - a)
            across_in(k, offset, 1 - a).start()

    everything = [*range(chunks), chunks]
    from_pair(0)
    from_level(0)
    for k in range(1, chunks - 1):
        from_pair(k)
        from_level(k)
    from_pair(chunks - 1)
    from_pair(chunks)
    from_level(chunks)
    from_level(chunks - 1)
    for k in everything:
        from_relays(k)

    for k in everything:
        for offset in range(-HOP, HOP + 1):
            for w in range(windows):
                across(k, place(k, offset, w), offset, w).wait_recv()

    gm_copy().wait_send()
    mean_pair().wait_send()
    mean_other().wait_send()

    @pl.when(has_back)
    def _():
        mean_back().wait_send()
        mean_diag().wait_send()

    for k in range(chunks):
        raw_outer(k).wait_send()
        raw_inner(k).wait_send()
        face(k).wait_send()

        @pl.when(has_back)
        def _():
            raw_back(k).wait_send()

        @pl.when(has_fwd)
        def _():
            raw_fwd(k).wait_send()

    for k in everything:
        for send in (y_other, y_self, fwd_self, fwd_other, back_self, fwd_relay):
            send(k).wait_send()

        @pl.when(relays_back(k))
        def _():
            y_relay_back(k).wait_send()

        @pl.when(relays_fwd(k))
        def _():
            y_relay_fwd(k).wait_send()

        if k == DETOUR:

            @pl.when(has_fwd)
            def _():
                fwd_detour(k).wait_send()

            @pl.when(has_back)
            def _():
                back_detour(k).wait_send()

        for p in range(2):
            own(k, p).wait()
        for offset in range(-HOP, HOP + 1):
            for w in range(windows):
                across(k, place(k, offset, w), offset, w).wait_send()


def tile_kernel(rows, cols, partners_ref, cand_ref, scale_ref, out_ref):
    i = pl.program_id(0)
    blocks = cand_ref.shape[2]
    block_rows = cand_ref.shape[4]
    windows = cand_ref.shape[1]
    slots = out_ref.shape[1]
    r = lax.axis_index("row")
    c = lax.axis_index("col")
    home = HOP * cols + c
    local = [cand_ref[home, w, i].T for w in range(windows)]
    left = [
        jnp.broadcast_to(scale_ref[home, w, pl.ds(i, 1), :], (block_rows, block_rows)).T
        for w in range(windows)
    ]
    for k in range(0, slots, 2):
        found = []
        for q in (k, k + 1):
            name = partners_ref[i, q]
            safe = jnp.maximum(name, 0)
            slab = safe // blocks
            distance = lax.rem(slab // cols - r + HOP + rows, rows)
            place = jnp.where(name >= 0, distance * cols + lax.rem(slab, cols), 0)
            found.append((name >= 0, place, lax.rem(safe, blocks)))
        for w in range(windows):
            right = jnp.concatenate([cand_ref[s, w, b] for _, s, b in found], axis=1)
            tiles = jnp.dot(local[w], right, preferred_element_type=jnp.float32)
            for n, (present, s, b) in enumerate(found):
                tile = tiles[:, n * block_rows : (n + 1) * block_rows]
                factor = jnp.where(present, scale_ref[s, w, pl.ds(b, 1), :], 0.0)
                out_ref[0, k + n, w] = (tile * left[w] * factor).astype(out_ref.dtype)


def on_device(rows, cols, bold, gm_index, partners):
    windows, frames, sx, sy, sz = bold.shape
    voxels = sx * sy * sz
    count = gm_index.shape[0]
    blocks, slots = partners.shape
    block_rows = count // blocks
    slabs = (2 * HOP + 1) * cols
    bf16, f32 = jnp.bfloat16, jnp.float32
    n = frames // CHUNKS
    dma = pltpu.SemaphoreType.DMA
    cand, scale = pl.pallas_call(
        functools.partial(panel_kernel, rows),
        out_shape=(
            jax.ShapeDtypeStruct((slabs, windows, blocks, frames, block_rows), bf16),
            jax.ShapeDtypeStruct((slabs, windows, blocks, block_rows), f32),
        ),
        in_specs=[pl.BlockSpec(memory_space=pltpu.VMEM), pl.BlockSpec(memory_space=pltpu.HBM)],
        out_specs=(pl.BlockSpec(memory_space=pl.ANY), pl.BlockSpec(memory_space=pl.ANY)),
        scratch_shapes=[
            pltpu.VMEM((windows, frames, sx, sy, sz), bf16),
            pltpu.VMEM((2 * sx + 2, frames, sy, sz), bf16),
            pltpu.VMEM((windows, sx, sy, sz), f32),
            pltpu.VMEM((2 * sx + 2, sy, sz), f32),
            pltpu.VMEM((2 * sx, sy, sz), f32),
            pltpu.VMEM((2 * sx, sy, sz), f32),
            pltpu.VMEM((2 * sx, sy, sz), f32),
            pltpu.VMEM((1, count), jnp.int32),
            pltpu.VMEM((2, voxels, count), bf16),
            pltpu.VMEM((2 * sx, n * sy, sz), f32),
            pltpu.VMEM((CHUNKS, 2 * sx, n, sz), f32),
            pltpu.VMEM((CHUNKS, 2 * sx, n, sz), f32),
            pltpu.VMEM((2, n, voxels), bf16),
            pltpu.VMEM((2, 1, count), f32),
            pltpu.VMEM((2, blocks, frames, block_rows), bf16),
            pltpu.VMEM((2, blocks, block_rows), f32),
            dma((4,)),
            dma((CHUNKS, 4)),
            dma((CHUNKS, 4)),
            dma((CHUNKS,)),
            dma((CHUNKS,)),
            dma((5,)),
            dma((5,)),
            dma((CHUNKS + 1, 2)),
            dma((CHUNKS + 1, 10)),
            dma((CHUNKS + 1, 2 * HOP + 1, 2)),
            dma((CHUNKS + 1, 2 * HOP + 1, 2)),
            dma((CHUNKS + 1, 2 * HOP + 1, 2)),
        ],
        compiler_params=pltpu.CompilerParams(
            collective_id=0, has_side_effects=True, vmem_limit_bytes=40 * 1024 * 1024
        ),
        name="panels",
    )(gm_index.reshape(1, count), bold)
    return pl.pallas_call(
        functools.partial(tile_kernel, rows, cols),
        out_shape=jax.ShapeDtypeStruct((blocks, slots, windows, block_rows, block_rows), bf16),
        grid_spec=pltpu.PrefetchScalarGridSpec(
            num_scalar_prefetch=1,
            grid=(blocks,),
            in_specs=[pl.BlockSpec(memory_space=pltpu.VMEM)] * 2,
            out_specs=pl.BlockSpec(
                (1, slots, windows, block_rows, block_rows), lambda i, names: (i, 0, 0, 0, 0)
            ),
        ),
        compiler_params=pltpu.CompilerParams(vmem_limit_bytes=40 * 1024 * 1024),
        name="tiles",
    )(partners, cand, scale)


def solution(mesh):
    rows, cols = mesh.shape["row"], mesh.shape["col"]
    in_specs = (P("subj", None, "row", "col", None), P(("row", "col")), P(("row", "col"), None))
    out_specs = P(("row", "col"), None, "subj", None, None)
    return jax.shard_map(
        functools.partial(on_device, rows, cols),
        mesh=mesh,
        in_specs=in_specs,
        out_specs=out_specs,
        check_vma=False,
    )
```

```python
import functools
import math

import jax
import jax.numpy as jnp
from jax import lax
from jax.experimental import pallas as pl
from jax.experimental.pallas import tpu as pltpu
from jax.sharding import PartitionSpec as P

HOP = 2
MESH = pl.DeviceIdType.MESH
CHUNKS = 4
DETOUR = 0

side_weight = math.exp(-0.5) / (1.0 + 2.0 * math.exp(-0.5))
centre_weight = 1.0 / (1.0 + 2.0 * math.exp(-0.5))
SPAN, SPAN_SIDE, SPAN_CENTRE = 135.0, 37.0, 61.0


def three(low, mid, high):
    return side_weight * (low + high) + centre_weight * mid


def panel_kernel(
    rows,
    gm_hbm,
    bold_ref,
    partners_ref,
    cand_ref,
    scale_ref,
    names_ref,
    gm_own,
    bold,
    ext,
    mean_own,
    mean_ext,
    mean_x,
    mean_face,
    mean_xy,
    gm_pair,
    pick,
    xf,
    face_out,
    face_in,
    lhs,
    square,
    panel,
    scale,
    local_sem,
    raw_send,
    raw_recv,
    face_send,
    face_recv,
    small_send,
    small_recv,
    own_sem,
    panel_send,
    panel_recv,
    across_send,
    across_recv,
):
    windows, frames, sx, sy, sz = bold_ref.shape
    count = gm_own.shape[1]
    blocks = panel.shape[1]
    chunks = face_in.shape[0]
    n = frames // chunks
    r = lax.axis_index("row")
    c = lax.axis_index("col")
    a = lax.rem(r, 2)
    ahead = 1 - 2 * a
    pair = r + ahead
    fwd = lax.rem(r + 2 * ahead + rows, rows)
    back = lax.rem(r - 2 * ahead + rows, rows)
    diag = lax.rem(r - ahead + rows, rows)
    other = {"col": 1 - c}
    to_pair, to_fwd, to_back, to_diag = {"row": pair}, {"row": fwd}, {"row": back}, {"row": diag}
    level = r + (rows - 2 * r - 1) * a
    has_fwd = level < rows - 2
    has_back = level > 0
    mine = 1 + 2 * a
    theirs = 3 - 2 * a
    back_edge = 5 * a
    fwd_edge = 5 - 5 * a

    barrier = pltpu.get_barrier_semaphore()
    for target in (to_pair, to_fwd, to_back, to_diag, other):
        pl.semaphore_signal(barrier, inc=1, device_id=target, device_id_type=MESH)

    def load(w):
        return pltpu.make_async_copy(bold_ref.at[w], bold.at[w], local_sem.at[w])

    def load_own(x):
        return pltpu.make_async_copy(bold_ref.at[a, :, x], ext.at[mine + x], local_sem.at[2 + x])

    def load_gm():
        return pltpu.make_async_copy(gm_hbm, gm_own, local_sem.at[4])

    def load_names():
        return pltpu.make_async_copy(partners_ref, names_ref, local_sem.at[5])

    load_gm().start()
    load_names().start()
    for w in range(windows):
        load(w).start()
    for x in range(sx):
        load_own(x).start()

    def remote(src, dst, send_sem, recv_sem, target):
        return pltpu.make_async_remote_copy(
            src_ref=src,
            dst_ref=dst,
            send_sem=send_sem,
            recv_sem=recv_sem,
            device_id=target,
            device_id_type=MESH,
        )

    def at(k):
        return pl.ds(pl.multiple_of(k * n, n), n)

    def raw_outer(k):
        return remote(
            bold_ref.at[1 - a, at(k), a], ext.at[mine + a, at(k)],
            raw_send.at[k, 0], raw_recv.at[k, 0], to_pair,
        )

    def raw_inner(k):
        return remote(
            bold_ref.at[1 - a, at(k), 1 - a], ext.at[mine + 1 - a, at(k)],
            raw_send.at[k, 1], raw_recv.at[k, 1], to_pair,
        )

    def raw_back(k):
        return remote(
            bold_ref.at[a, at(k), a], ext.at[fwd_edge, at(k)],
            raw_send.at[k, 2], raw_recv.at[k, 2], to_back,
        )

    def raw_fwd(k):
        return remote(
            ext.at[theirs + 1 - a, at(k)], ext.at[back_edge, at(k)],
            raw_send.at[k, 3], raw_recv.at[k, 3], to_fwd,
        )

    def gm_copy():
        return remote(gm_hbm, gm_pair, small_send.at[0], small_recv.at[0], to_pair)

    def mean_pair():
        return remote(
            mean_own.at[1 - a], mean_ext.at[pl.ds(mine, sx)], small_send.at[1], small_recv.at[1], to_pair
        )

    def mean_back():
        return remote(
            mean_own.at[a, a], mean_ext.at[fwd_edge], small_send.at[2], small_recv.at[2], to_back
        )

    def mean_diag():
        return remote(
            mean_own.at[1 - a, a], mean_ext.at[fwd_edge], small_send.at[3], small_recv.at[3], to_diag
        )

    def mean_other():
        return remote(mean_x, mean_face, small_send.at[4], small_recv.at[4], other)

    def face(k):
        return remote(face_out.at[k], face_in.at[k], face_send.at[k], face_recv.at[k], other)

    def build(gm, p):
        tile = lax.shift_right_arithmetic(gm, 7)
        lane = jnp.bitwise_and(gm, sz - 1)
        z = lax.broadcasted_iota(jnp.int32, (sz, count), 0)

        def fill(step, carry):
            start = pl.multiple_of(step * sz, sz)
            away = jnp.abs(z - jnp.where(tile == step, lane, 4 * sz))
            weight = jnp.where(away == 0, SPAN_CENTRE, jnp.where(away == 1, SPAN_SIDE, 0.0))
            pick[p, pl.ds(start, sz), :] = weight.astype(jnp.bfloat16)
            return carry

        lax.fori_loop(0, sx * sy, fill, 0)

    @pl.when(jnp.logical_not(has_back))
    def _():
        ext[back_edge] = jnp.zeros(ext.shape[1:], ext.dtype)
        mean_ext[back_edge] = jnp.zeros(mean_ext.shape[1:], mean_ext.dtype)

    @pl.when(jnp.logical_not(has_fwd))
    def _():
        ext[fwd_edge] = jnp.zeros(ext.shape[1:], ext.dtype)
        mean_ext[fwd_edge] = jnp.zeros(mean_ext.shape[1:], mean_ext.dtype)

    pl.semaphore_wait(barrier, 5)

    gm_copy().start()
    raw_outer(0).start()
    raw_inner(0).start()

    @pl.when(has_back)
    def _():
        raw_back(0).start()

    for w in range(windows):
        load(w).wait()
    part = 16

    def add_frames(step, total):
        here = bold[:, pl.ds(step * part, part)].astype(jnp.float32)
        return total + jnp.sum(here, axis=1)

    total = lax.fori_loop(
        0, frames // part, add_frames, jnp.zeros((windows, sx, sy, sz), jnp.float32)
    )
    mean_own[...] = total * (1.0 / frames)
    mean_pair().start()

    @pl.when(has_back)
    def _():
        mean_back().start()
        mean_diag().start()

    for k in range(1, chunks):
        raw_outer(k).start()
    for k in range(1, chunks):
        raw_inner(k).start()
    for k in range(1, chunks):

        @pl.when(has_back)
        def _():
            raw_back(k).start()

    mean_ext[pl.ds(mine, sx)] = mean_own[a]

    load_gm().wait()
    build(gm_own[...], a)

    def relay_raw(k):
        raw_outer(k).wait_recv()

        @pl.when(has_fwd)
        def _():
            raw_fwd(k).start()

    relay_raw(0)
    gm_copy().wait_recv()
    build(gm_pair[...], 1 - a)

    mean_pair().wait_recv()

    @pl.when(has_fwd)
    def _():
        mean_back().wait_recv()

    @pl.when(has_back)
    def _():
        remote(
            mean_own.at[1 - a, a], mean_ext.at[back_edge], small_send.at[3], small_recv.at[3], to_diag
        ).wait_recv()

    for l in range(2 * sx):
        mean_x[l] = three(mean_ext[l], mean_ext[l + 1], mean_ext[l + 2])
    mean_other().start()
    mean_other().wait_recv()
    nothing = jnp.zeros((1, sz), jnp.float32)
    for l in range(2 * sx):
        inner = mean_x[l]
        first = jnp.where(c == 1, mean_face[l, sy - 1 : sy, :], nothing)
        last = jnp.where(c == 0, mean_face[l, 0:1, :], nothing)
        low = jnp.concatenate([first, inner[: sy - 1]], axis=0)
        high = jnp.concatenate([inner[1:], last], axis=0)
        mean_xy[l] = three(low, inner, high)
    square[...] = jnp.zeros_like(square)
    load_names().wait()
    for x in range(sx):
        load_own(x).wait()

    def slot(offset, col):
        return (offset + HOP) * 2 + col

    def made(k, p):
        if isinstance(k, int) and k == chunks:
            return scale.at[p]
        return panel.at[p, :, at(k), :]

    def place(k, offset, w):
        if isinstance(k, int) and k == chunks:
            return scale_ref.at[slot(offset, c), w]
        return cand_ref.at[slot(offset, c), w, :, at(k), :]

    def piece(k, src, offset, w, which, target):
        return remote(
            src, place(k, offset, w),
            panel_send.at[k, which], panel_recv.at[k, offset + HOP, w], target,
        )

    def y_other(k):
        return piece(k, made(k, 1 - a), 0 * a, a, 0, to_pair)

    def y_self(k):
        return piece(k, made(k, a), -ahead, a, 1, to_pair)

    def fwd_self(k):
        return piece(k, made(k, a), -2 * ahead, a, 2, to_fwd)

    def fwd_other(k):
        return piece(k, made(k, 1 - a), -ahead, a, 3, to_fwd)

    def back_self(k):
        return piece(k, made(k, a), 2 * ahead, a, 4, to_back)

    def fwd_relay(k):
        return piece(k, place(k, 0 * a, 1 - a), -2 * ahead, 1 - a, 5, to_fwd)

    def y_relay_back(k):
        return piece(k, place(k, -ahead, a), -2 * ahead, a, 6, to_pair)

    def y_relay_fwd(k):
        return piece(k, place(k, 2 * ahead, a), ahead, a, 7, to_pair)

    def fwd_detour(k):
        return piece(k, place(k, ahead, 1 - a), -ahead, 1 - a, 8, to_fwd)

    def back_detour(k):
        return piece(k, place(k, 0 * a, 1 - a), 2 * ahead, 1 - a, 9, to_back)

    def arrived(k, offset, w):
        remote(
            place(k, offset, w), place(k, offset, w),
            panel_send.at[k, 0], panel_recv.at[k, offset + HOP, w], to_pair,
        ).wait_recv()

    def across(k, src, offset, w):
        return remote(
            src, place(k, offset, w),
            across_send.at[k, offset + HOP, w], across_recv.at[k, offset + HOP, w], other,
        )

    def across_own(k, p):
        return across(k, made(k, p), p - a, a)

    def across_in(k, offset, w):
        return across(k, place(k, offset, w), offset, w)

    def own(k, p):
        return pltpu.make_async_copy(made(k, p), place(k, p - a, a), own_sem.at[k, p])

    def emit(k):
        fwd_self(k).start()
        y_other(k).start()
        back_self(k).start()
        y_self(k).start()
        fwd_other(k).start()
        for p in range(2):
            own(k, p).start()
            across_own(k, p).start()

    step_frames = 8

    def compute(k, carry):

        raw_inner(k).wait_recv()

        @pl.when(has_fwd)
        def _():
            raw_back(k).wait_recv()

        @pl.when(has_back)
        def _():
            raw_fwd(k).wait_recv()

        def filter_x(step, inner):
            here = pl.ds(k * n + step * step_frames, step_frames)
            flat = pl.ds(pl.multiple_of(step * step_frames * sy, step_frames * sy), step_frames * sy)
            layer = [ext[l, here].astype(jnp.float32) for l in range(2 * sx + 2)]
            for l in range(2 * sx):
                xf[l, flat, :] = three(layer[l], layer[l + 1], layer[l + 2]).reshape(step_frames * sy, sz)
            return inner

        lax.fori_loop(0, n // step_frames, filter_x, 0)

        edge = (sy - 1) * (1 - c)
        for l in range(2 * sx):
            face_out[k, l] = xf[l, pl.ds(edge, n, stride=sy), :]
        face(k).start()

        @pl.when(k == 0)
        def _():
            relay_raw(1)

        def row_of(l, y):
            return xf[l, pl.ds(y, n, stride=sy), :]

        def finish(l, y, low, mid, high):
            value = three(low, mid, high) - mean_xy[l, y : y + 1, :]
            start = ((l % sx) * sy + y) * sz
            lhs[l // sx, :, start : start + sz] = value.astype(jnp.bfloat16)

        for l in range(2 * sx):
            low, mid = row_of(l, 0), row_of(l, 1)
            for y in range(1, sy - 1):
                high = row_of(l, y + 1)
                finish(l, y, low, mid, high)
                low, mid = mid, high
        face(k).wait_recv()
        for l in range(2 * sx):
            outside = face_in[k, l]
            finish(l, 0, jnp.where(c == 1, outside, 0.0), row_of(l, 0), row_of(l, 1))
            finish(l, sy - 1, row_of(l, sy - 2), row_of(l, sy - 1), jnp.where(c == 0, outside, 0.0))

        wide = 2 * sz
        for p in range(2):
            for j in range(count // wide):
                cols = slice(j * wide, (j + 1) * wide)
                got = jnp.dot(lhs[p], pick[p, :, cols], preferred_element_type=jnp.float32)
                square[p, :, cols] += jnp.sum(got * got, axis=0, keepdims=True)
                small = got.astype(jnp.bfloat16)
                panel[p, 2 * j, at(k), :] = small[:, :sz]
                panel[p, 2 * j + 1, at(k), :] = small[:, sz:]
        emit(k)

        @pl.when(k == 0)
        def _():
            for later in range(2, chunks):
                relay_raw(later)

        return carry

    lax.fori_loop(0, chunks, compute, 0)

    for p in range(2):
        value = lax.rsqrt(square[p] + 1e-05 * frames * SPAN * SPAN)
        for b in range(blocks):
            scale[p, b : b + 1, :] = value[:, b * sz : (b + 1) * sz]
    emit(chunks)

    def relays_back(k):
        return jnp.logical_not(has_back) if k == DETOUR else r >= 0

    def relays_fwd(k):
        return jnp.logical_not(has_fwd) if k == DETOUR else r >= 0

    def from_pair(k):
        arrived(k, 0 * a, 1 - a)
        fwd_relay(k).start()
        if k == DETOUR:

            @pl.when(has_back)
            def _():
                back_detour(k).start()

        across_in(k, 0 * a, 1 - a).start()
        arrived(k, ahead, 1 - a)
        if k == DETOUR:

            @pl.when(has_fwd)
            def _():
                fwd_detour(k).start()

        across_in(k, ahead, 1 - a).start()

    def from_level(k):
        arrived(k, -ahead, a)

        @pl.when(relays_back(k))
        def _():
            y_relay_back(k).start()

        across_in(k, -ahead, a).start()
        arrived(k, 2 * ahead, a)

        @pl.when(relays_fwd(k))
        def _():
            y_relay_fwd(k).start()

        across_in(k, 2 * ahead, a).start()
        arrived(k, -2 * ahead, a)
        across_in(k, -2 * ahead, a).start()

    def from_relays(k):
        for offset in (-2 * ahead, -ahead, 2 * ahead):
            arrived(k, offset, 1 - a)
            across_in(k, offset, 1 - a).start()

    everything = [*range(chunks), chunks]
    from_pair(0)
    from_level(0)
    for k in range(1, chunks - 1):
        from_pair(k)
        from_level(k)
    from_pair(chunks - 1)
    from_pair(chunks)
    from_level(chunks)
    from_level(chunks - 1)
    for k in everything:
        from_relays(k)

    for k in everything:
        for offset in range(-HOP, HOP + 1):
            for w in range(windows):
                across(k, place(k, offset, w), offset, w).wait_recv()

    gm_copy().wait_send()
    mean_pair().wait_send()
    mean_other().wait_send()

    @pl.when(has_back)
    def _():
        mean_back().wait_send()
        mean_diag().wait_send()

    for k in range(chunks):
        raw_outer(k).wait_send()
        raw_inner(k).wait_send()
        face(k).wait_send()

        @pl.when(has_back)
        def _():
            raw_back(k).wait_send()

        @pl.when(has_fwd)
        def _():
            raw_fwd(k).wait_send()

    for k in everything:
        for send in (y_other, y_self, fwd_self, fwd_other, back_self, fwd_relay):
            send(k).wait_send()

        @pl.when(relays_back(k))
        def _():
            y_relay_back(k).wait_send()

        @pl.when(relays_fwd(k))
        def _():
            y_relay_fwd(k).wait_send()

        if k == DETOUR:

            @pl.when(has_fwd)
            def _():
                fwd_detour(k).wait_send()

            @pl.when(has_back)
            def _():
                back_detour(k).wait_send()

        for p in range(2):
            own(k, p).wait()
        for offset in range(-HOP, HOP + 1):
            for w in range(windows):
                across(k, place(k, offset, w), offset, w).wait_send()


def tile_kernel(rows, cols, names_ref, cand_ref, scale_ref, out_ref, buffer, out_sem):
    blocks = cand_ref.shape[2]
    block_rows = cand_ref.shape[4]
    windows = cand_ref.shape[1]
    slots = out_ref.shape[1]
    halves = out_sem.shape[1]
    half = slots // halves
    r = lax.axis_index("row")
    c = lax.axis_index("col")
    home = HOP * cols + c

    def copy(i, h):
        part = pl.ds(h * half, half)
        return pltpu.make_async_copy(buffer.at[i, part], out_ref.at[i, part], out_sem.at[i, h])

    for i in range(blocks):
        local = [cand_ref[home, w, i].T for w in range(windows)]
        left = [
            jnp.broadcast_to(scale_ref[home, w, i : i + 1, :], (block_rows, block_rows)).T
            for w in range(windows)
        ]
        for k in range(0, slots, 2):
            found = []
            for q in (k, k + 1):
                name = names_ref[i, q]
                safe = jnp.maximum(name, 0)
                slab = safe // blocks
                distance = lax.rem(slab // cols - r + HOP + rows, rows)
                place = jnp.where(name >= 0, distance * cols + lax.rem(slab, cols), 0)
                found.append((name >= 0, place, lax.rem(safe, blocks)))
            for w in range(windows):
                right = jnp.concatenate([cand_ref[s, w, b] for _, s, b in found], axis=1)
                tiles = jnp.dot(local[w], right, preferred_element_type=jnp.float32)
                for n, (present, s, b) in enumerate(found):
                    tile = tiles[:, n * block_rows : (n + 1) * block_rows]
                    factor = jnp.where(present, scale_ref[s, w, pl.ds(b, 1), :], 0.0)
                    buffer[i, k + n, w] = (tile * left[w] * factor).astype(out_ref.dtype)
            if (k + 2) % half == 0:
                copy(i, (k + 2) // half - 1).start()
    for i in range(blocks):
        for h in range(halves):
            copy(i, h).wait()


def on_device(rows, cols, bold, gm_index, partners):
    windows, frames, sx, sy, sz = bold.shape
    voxels = sx * sy * sz
    count = gm_index.shape[0]
    blocks, slots = partners.shape
    block_rows = count // blocks
    slabs = (2 * HOP + 1) * cols
    bf16, f32 = jnp.bfloat16, jnp.float32
    n = frames // CHUNKS
    dma = pltpu.SemaphoreType.DMA
    in_hbm = [
        pltpu.with_memory_space_constraint(x, pltpu.HBM)
        for x in (gm_index.reshape(1, count), bold, partners)
    ]
    cand, scale, names = pl.pallas_call(
        functools.partial(panel_kernel, rows),
        out_shape=(
            jax.ShapeDtypeStruct((slabs, windows, blocks, frames, block_rows), bf16),
            jax.ShapeDtypeStruct((slabs, windows, blocks, block_rows), f32),
            jax.ShapeDtypeStruct(partners.shape, partners.dtype),
        ),
        in_specs=[pl.BlockSpec(memory_space=pltpu.HBM)] * 3,
        out_specs=(pl.BlockSpec(memory_space=pl.ANY),) * 3,
        scratch_shapes=[
            pltpu.VMEM((1, count), jnp.int32),
            pltpu.VMEM((windows, frames, sx, sy, sz), bf16),
            pltpu.VMEM((2 * sx + 2, frames, sy, sz), bf16),
            pltpu.VMEM((windows, sx, sy, sz), f32),
            pltpu.VMEM((2 * sx + 2, sy, sz), f32),
            pltpu.VMEM((2 * sx, sy, sz), f32),
            pltpu.VMEM((2 * sx, sy, sz), f32),
            pltpu.VMEM((2 * sx, sy, sz), f32),
            pltpu.VMEM((1, count), jnp.int32),
            pltpu.VMEM((2, voxels, count), bf16),
            pltpu.VMEM((2 * sx, n * sy, sz), f32),
            pltpu.VMEM((CHUNKS, 2 * sx, n, sz), f32),
            pltpu.VMEM((CHUNKS, 2 * sx, n, sz), f32),
            pltpu.VMEM((2, n, voxels), bf16),
            pltpu.VMEM((2, 1, count), f32),
            pltpu.VMEM((2, blocks, frames, block_rows), bf16),
            pltpu.VMEM((2, blocks, block_rows), f32),
            dma((6,)),
            dma((CHUNKS, 4)),
            dma((CHUNKS, 4)),
            dma((CHUNKS,)),
            dma((CHUNKS,)),
            dma((5,)),
            dma((5,)),
            dma((CHUNKS + 1, 2)),
            dma((CHUNKS + 1, 10)),
            dma((CHUNKS + 1, 2 * HOP + 1, 2)),
            dma((CHUNKS + 1, 2 * HOP + 1, 2)),
            dma((CHUNKS + 1, 2 * HOP + 1, 2)),
        ],
        compiler_params=pltpu.CompilerParams(
            collective_id=0, has_side_effects=True, vmem_limit_bytes=40 * 1024 * 1024
        ),
        name="panels",
    )(*in_hbm)
    out_shape = (blocks, slots, windows, block_rows, block_rows)
    return pl.pallas_call(
        functools.partial(tile_kernel, rows, cols),
        out_shape=jax.ShapeDtypeStruct(out_shape, bf16),
        in_specs=[pl.BlockSpec(memory_space=pltpu.SMEM)]
        + [pl.BlockSpec(memory_space=pltpu.VMEM)] * 2,
        out_specs=pl.BlockSpec(memory_space=pl.ANY),
        scratch_shapes=[pltpu.VMEM(out_shape, bf16), dma((blocks, 2))],
        compiler_params=pltpu.CompilerParams(vmem_limit_bytes=40 * 1024 * 1024),
        name="tiles",
    )(names, cand, scale)


def solution(mesh):
    rows, cols = mesh.shape["row"], mesh.shape["col"]
    in_specs = (P("subj", None, "row", "col", None), P(("row", "col")), P(("row", "col"), None))
    out_specs = P(("row", "col"), None, "subj", None, None)
    return jax.shard_map(
        functools.partial(on_device, rows, cols),
        mesh=mesh,
        in_specs=in_specs,
        out_specs=out_specs,
        check_vma=False,
    )
```

```python
import functools
import math

import jax
import jax.numpy as jnp
from jax import lax
from jax.experimental import pallas as pl
from jax.experimental.pallas import tpu as pltpu
from jax.sharding import PartitionSpec as P

HOP = 2
MESH = pl.DeviceIdType.MESH
PARTS = (3, 4, 5, 4)
CHUNKS = len(PARTS)
DETOUR = (1,)
WRAP_DETOUR = ()

side_weight = math.exp(-0.5) / (1.0 + 2.0 * math.exp(-0.5))
centre_weight = 1.0 / (1.0 + 2.0 * math.exp(-0.5))
SPAN, SPAN_SIDE, SPAN_CENTRE = 135.0, 37.0, 61.0


def three(low, mid, high):
    return side_weight * (low + high) + centre_weight * mid


def panel_kernel(
    rows,
    gm_hbm,
    bold_ref,
    partners_ref,
    cand_ref,
    scale_ref,
    names_ref,
    gm_own,
    bold,
    ext,
    mean_own,
    mean_ext,
    mean_x,
    mean_face,
    mean_xy,
    gm_pair,
    pick,
    xf,
    face_out,
    face_in,
    lhs,
    square,
    panel,
    scale,
    local_sem,
    raw_send,
    raw_recv,
    face_send,
    face_recv,
    small_send,
    small_recv,
    own_sem,
    panel_send,
    panel_recv,
    across_send,
    across_recv,
):
    windows, frames, sx, sy, sz = bold_ref.shape
    count = gm_own.shape[1]
    blocks = panel.shape[1]
    chunks = CHUNKS
    sizes = [p * frames // 16 for p in PARTS]
    r = lax.axis_index("row")
    c = lax.axis_index("col")
    a = lax.rem(r, 2)
    ahead = 1 - 2 * a
    pair = r + ahead
    fwd = lax.rem(r + 2 * ahead + rows, rows)
    back = lax.rem(r - 2 * ahead + rows, rows)
    diag = lax.rem(r - ahead + rows, rows)
    other = {"col": 1 - c}
    to_pair, to_fwd, to_back, to_diag = {"row": pair}, {"row": fwd}, {"row": back}, {"row": diag}
    level = r + (rows - 2 * r - 1) * a
    has_fwd = level < rows - 2
    has_back = level > 0
    mine = 1 + 2 * a
    theirs = 3 - 2 * a
    back_edge = 5 * a
    fwd_edge = 5 - 5 * a

    barrier = pltpu.get_barrier_semaphore()
    for target in (to_pair, to_fwd, to_back, to_diag, other):
        pl.semaphore_signal(barrier, inc=1, device_id=target, device_id_type=MESH)

    def load(w):
        return pltpu.make_async_copy(bold_ref.at[w], bold.at[w], local_sem.at[w])

    def load_own(x):
        return pltpu.make_async_copy(bold_ref.at[a, :, x], ext.at[mine + x], local_sem.at[2 + x])

    def load_gm():
        return pltpu.make_async_copy(gm_hbm, gm_own, local_sem.at[4])

    def load_names():
        return pltpu.make_async_copy(partners_ref, names_ref, local_sem.at[5])

    load_gm().start()
    load_names().start()
    for w in range(windows):
        load(w).start()
    for x in range(sx):
        load_own(x).start()

    def remote(src, dst, send_sem, recv_sem, target):
        return pltpu.make_async_remote_copy(
            src_ref=src,
            dst_ref=dst,
            send_sem=send_sem,
            recv_sem=recv_sem,
            device_id=target,
            device_id_type=MESH,
        )

    def at(k):
        return pl.ds(sum(sizes[:k]), sizes[k])

    def raw_outer(k):
        return remote(
            bold_ref.at[1 - a, at(k), a], ext.at[mine + a, at(k)],
            raw_send.at[k, 0], raw_recv.at[k, 0], to_pair,
        )

    def raw_inner(k):
        return remote(
            bold_ref.at[1 - a, at(k), 1 - a], ext.at[mine + 1 - a, at(k)],
            raw_send.at[k, 1], raw_recv.at[k, 1], to_pair,
        )

    def raw_back(k):
        return remote(
            bold_ref.at[a, at(k), a], ext.at[fwd_edge, at(k)],
            raw_send.at[k, 2], raw_recv.at[k, 2], to_back,
        )

    def raw_fwd(k):
        return remote(
            ext.at[theirs + 1 - a, at(k)], ext.at[back_edge, at(k)],
            raw_send.at[k, 3], raw_recv.at[k, 3], to_fwd,
        )

    def gm_copy():
        return remote(gm_hbm, gm_pair, small_send.at[0], small_recv.at[0], to_pair)

    def mean_pair():
        return remote(
            mean_own.at[1 - a], mean_ext.at[pl.ds(mine, sx)], small_send.at[1], small_recv.at[1], to_pair
        )

    def mean_back():
        return remote(
            mean_own.at[a, a], mean_ext.at[fwd_edge], small_send.at[2], small_recv.at[2], to_back
        )

    def mean_diag():
        return remote(
            mean_own.at[1 - a, a], mean_ext.at[fwd_edge], small_send.at[3], small_recv.at[3], to_diag
        )

    def mean_other():
        return remote(mean_x, mean_face, small_send.at[4], small_recv.at[4], other)

    def face(k):
        part = pl.ds(0, sizes[k])
        return remote(face_out.at[k, :, part], face_in.at[k, :, part], face_send.at[k], face_recv.at[k], other)

    def build(gm, p):
        tile = lax.shift_right_arithmetic(gm, 7)
        lane = jnp.bitwise_and(gm, sz - 1)
        z = lax.broadcasted_iota(jnp.int32, (sz, count), 0).astype(jnp.float32).astype(jnp.bfloat16)
        centre = jnp.asarray(SPAN_CENTRE, jnp.bfloat16)
        drop = jnp.asarray(SPAN_CENTRE - SPAN_SIDE, jnp.bfloat16)

        def fill(step, carry):
            start = pl.multiple_of(step * sz, sz)
            at_tile = jnp.where(tile == step, lane, 4 * sz).astype(jnp.float32).astype(jnp.bfloat16)
            away = z - at_tile
            pick[p, pl.ds(start, sz), :] = jnp.maximum(centre - drop * (away * away), 0)
            return carry

        lax.fori_loop(0, sx * sy, fill, 0)

    @pl.when(jnp.logical_not(has_back))
    def _():
        ext[back_edge] = jnp.zeros(ext.shape[1:], ext.dtype)
        mean_ext[back_edge] = jnp.zeros(mean_ext.shape[1:], mean_ext.dtype)

    @pl.when(jnp.logical_not(has_fwd))
    def _():
        ext[fwd_edge] = jnp.zeros(ext.shape[1:], ext.dtype)
        mean_ext[fwd_edge] = jnp.zeros(mean_ext.shape[1:], mean_ext.dtype)

    load_gm().wait()
    build(gm_own[...], a)

    pl.semaphore_wait(barrier, 5)

    gm_copy().start()
    raw_outer(0).start()
    raw_inner(0).start()

    @pl.when(has_back)
    def _():
        raw_back(0).start()

    for w in range(windows):
        load(w).wait()
    part = 16

    def add_frames(step, total):
        here = bold[:, pl.ds(step * part, part)].astype(jnp.float32)
        return total + jnp.sum(here, axis=1)

    total = lax.fori_loop(
        0, frames // part, add_frames, jnp.zeros((windows, sx, sy, sz), jnp.float32)
    )
    mean_own[...] = total * (1.0 / frames)
    mean_pair().start()

    @pl.when(has_back)
    def _():
        mean_back().start()
        mean_diag().start()

    for k in range(1, chunks):
        raw_outer(k).start()
    for k in range(1, chunks):
        raw_inner(k).start()
    for k in range(1, chunks):

        @pl.when(has_back)
        def _():
            raw_back(k).start()

    mean_ext[pl.ds(mine, sx)] = mean_own[a]

    def relay_raw(k):
        raw_outer(k).wait_recv()

        @pl.when(has_fwd)
        def _():
            raw_fwd(k).start()

    relay_raw(0)
    gm_copy().wait_recv()
    build(gm_pair[...], 1 - a)

    mean_pair().wait_recv()

    @pl.when(has_fwd)
    def _():
        mean_back().wait_recv()

    @pl.when(has_back)
    def _():
        remote(
            mean_own.at[1 - a, a], mean_ext.at[back_edge], small_send.at[3], small_recv.at[3], to_diag
        ).wait_recv()

    for l in range(2 * sx):
        mean_x[l] = three(mean_ext[l], mean_ext[l + 1], mean_ext[l + 2])
    mean_other().start()
    mean_other().wait_recv()
    nothing = jnp.zeros((1, sz), jnp.float32)
    for l in range(2 * sx):
        inner = mean_x[l]
        first = jnp.where(c == 1, mean_face[l, sy - 1 : sy, :], nothing)
        last = jnp.where(c == 0, mean_face[l, 0:1, :], nothing)
        low = jnp.concatenate([first, inner[: sy - 1]], axis=0)
        high = jnp.concatenate([inner[1:], last], axis=0)
        mean_xy[l] = three(low, inner, high)
    square[...] = jnp.zeros_like(square)
    load_names().wait()
    for x in range(sx):
        load_own(x).wait()

    def slot(offset, col):
        return (offset + HOP) * 2 + col

    def made(k, p):
        if k == chunks:
            return scale.at[p]
        return panel.at[p, :, at(k), :]

    def place(k, offset, w):
        if k == chunks:
            return scale_ref.at[slot(offset, c), w]
        return cand_ref.at[slot(offset, c), w, :, at(k), :]

    def piece(k, src, offset, w, which, target):
        return remote(
            src, place(k, offset, w),
            panel_send.at[k, which], panel_recv.at[k, offset + HOP, w], target,
        )

    def y_other(k):
        return piece(k, made(k, 1 - a), 0 * a, a, 0, to_pair)

    def y_self(k):
        return piece(k, made(k, a), -ahead, a, 1, to_pair)

    def fwd_self(k):
        return piece(k, made(k, a), -2 * ahead, a, 2, to_fwd)

    def fwd_other(k):
        return piece(k, made(k, 1 - a), -ahead, a, 3, to_fwd)

    def back_self(k):
        return piece(k, made(k, a), 2 * ahead, a, 4, to_back)

    def fwd_relay(k):
        return piece(k, place(k, 0 * a, 1 - a), -2 * ahead, 1 - a, 5, to_fwd)

    def y_relay_back(k):
        return piece(k, place(k, -ahead, a), -2 * ahead, a, 6, to_pair)

    def y_relay_fwd(k):
        return piece(k, place(k, 2 * ahead, a), ahead, a, 7, to_pair)

    def fwd_detour(k):
        return piece(k, place(k, ahead, 1 - a), -ahead, 1 - a, 8, to_fwd)

    def back_detour(k):
        return piece(k, place(k, 0 * a, 1 - a), 2 * ahead, 1 - a, 9, to_back)

    def arrived(k, offset, w):
        remote(
            place(k, offset, w), place(k, offset, w),
            panel_send.at[k, 0], panel_recv.at[k, offset + HOP, w], to_pair,
        ).wait_recv()

    def across(k, src, offset, w):
        return remote(
            src, place(k, offset, w),
            across_send.at[k, offset + HOP, w], across_recv.at[k, offset + HOP, w], other,
        )

    def across_own(k, p):
        return across(k, made(k, p), p - a, a)

    def across_in(k, offset, w):
        return across(k, place(k, offset, w), offset, w)

    def own(k, p):
        return pltpu.make_async_copy(made(k, p), place(k, p - a, a), own_sem.at[k, p])

    def emit(k):
        fwd_self(k).start()
        y_other(k).start()
        back_self(k).start()
        y_self(k).start()
        fwd_other(k).start()
        for p in range(2):
            own(k, p).start()
            across_own(k, p).start()

    step_frames = 8

    def compute(k):
        n = sizes[k]
        begin = sum(sizes[:k])
        raw_inner(k).wait_recv()

        @pl.when(has_fwd)
        def _():
            raw_back(k).wait_recv()

        @pl.when(has_back)
        def _():
            raw_fwd(k).wait_recv()

        def filter_x(step, inner):
            here = pl.ds(begin + step * step_frames, step_frames)
            flat = pl.ds(pl.multiple_of(step * step_frames * sy, step_frames * sy), step_frames * sy)
            layer = [ext[l, here].astype(jnp.float32) for l in range(2 * sx + 2)]
            for l in range(2 * sx):
                xf[l, flat, :] = three(layer[l], layer[l + 1], layer[l + 2]).reshape(step_frames * sy, sz)
            return inner

        lax.fori_loop(0, n // step_frames, filter_x, 0)

        edge = (sy - 1) * (1 - c)
        for l in range(2 * sx):
            face_out[k, l, :n] = xf[l, pl.ds(edge, n, stride=sy), :]
        face(k).start()

        if k == 0:
            relay_raw(1)

        def row_of(l, y):
            return xf[l, pl.ds(y, n, stride=sy), :]

        def finish(l, y, low, mid, high):
            value = three(low, mid, high) - mean_xy[l, y : y + 1, :]
            start = ((l % sx) * sy + y) * sz
            lhs[l // sx, :n, start : start + sz] = value.astype(jnp.bfloat16)

        for l in range(2 * sx):
            low, mid = row_of(l, 0), row_of(l, 1)
            for y in range(1, sy - 1):
                high = row_of(l, y + 1)
                finish(l, y, low, mid, high)
                low, mid = mid, high
        face(k).wait_recv()
        for l in range(2 * sx):
            outside = face_in[k, l, :n]
            finish(l, 0, jnp.where(c == 1, outside, 0.0), row_of(l, 0), row_of(l, 1))
            finish(l, sy - 1, row_of(l, sy - 2), row_of(l, sy - 1), jnp.where(c == 0, outside, 0.0))

        wide = 2 * sz
        for p in range(2):
            for j in range(count // wide):
                cols = slice(j * wide, (j + 1) * wide)
                got = jnp.dot(lhs[p, :n], pick[p, :, cols], preferred_element_type=jnp.float32)
                square[p, :, cols] += jnp.sum(got * got, axis=0, keepdims=True)
                small = got.astype(jnp.bfloat16)
                panel[p, 2 * j, at(k), :] = small[:, :sz]
                panel[p, 2 * j + 1, at(k), :] = small[:, sz:]
        emit(k)

        if k == 0:
            for later in range(2, chunks):
                relay_raw(later)

    for k in range(chunks):
        compute(k)

    for p in range(2):
        value = lax.rsqrt(square[p] + 1e-05 * frames * SPAN * SPAN)
        for b in range(blocks):
            scale[p, b : b + 1, :] = value[:, b * sz : (b + 1) * sz]
    emit(chunks)

    def detours(k, inside):
        near = inside if k in DETOUR else r < 0
        far = jnp.logical_not(inside) if k in WRAP_DETOUR else r < 0
        return jnp.logical_or(near, far)

    def relays_back(k):
        return jnp.logical_not(detours(k, has_back))

    def relays_fwd(k):
        return jnp.logical_not(detours(k, has_fwd))

    def from_pair(k):
        arrived(k, 0 * a, 1 - a)
        fwd_relay(k).start()
        @pl.when(detours(k, has_back))
        def _():
            back_detour(k).start()

        across_in(k, 0 * a, 1 - a).start()
        arrived(k, ahead, 1 - a)
        @pl.when(detours(k, has_fwd))
        def _():
            fwd_detour(k).start()

        across_in(k, ahead, 1 - a).start()

    def from_level(k):
        arrived(k, -ahead, a)

        @pl.when(relays_back(k))
        def _():
            y_relay_back(k).start()

        across_in(k, -ahead, a).start()
        arrived(k, 2 * ahead, a)

        @pl.when(relays_fwd(k))
        def _():
            y_relay_fwd(k).start()

        across_in(k, 2 * ahead, a).start()
        arrived(k, -2 * ahead, a)
        across_in(k, -2 * ahead, a).start()

    def from_relays(k):
        for offset in (-2 * ahead, -ahead, 2 * ahead):
            arrived(k, offset, 1 - a)
            across_in(k, offset, 1 - a).start()

    from_pair(0)
    from_level(0)
    for k in range(1, chunks - 1):
        from_pair(k)
        from_level(k)
    from_pair(chunks - 1)
    from_pair(chunks)
    from_level(chunks)
    from_level(chunks - 1)

    gm_copy().wait_send()
    mean_pair().wait_send()
    mean_other().wait_send()

    @pl.when(has_back)
    def _():
        mean_back().wait_send()
        mean_diag().wait_send()

    for k in range(chunks):
        raw_outer(k).wait_send()
        raw_inner(k).wait_send()
        face(k).wait_send()

        @pl.when(has_back)
        def _():
            raw_back(k).wait_send()

        @pl.when(has_fwd)
        def _():
            raw_fwd(k).wait_send()

    def settle(k):
        for send in (y_other, y_self, fwd_self, fwd_other, back_self, fwd_relay):
            send(k).wait_send()
        for p in range(2):
            own(k, p).wait()

        @pl.when(relays_back(k))
        def _():
            y_relay_back(k).wait_send()

        @pl.when(relays_fwd(k))
        def _():
            y_relay_fwd(k).wait_send()

        @pl.when(detours(k, has_fwd))
        def _():
            fwd_detour(k).wait_send()

        @pl.when(detours(k, has_back))
        def _():
            back_detour(k).wait_send()

        for offset in range(-HOP, HOP + 1):
            for w in range(windows):
                copy = across(k, place(k, offset, w), offset, w)
                copy.wait_send()
                copy.wait_recv()

    order = [*range(chunks - 1), chunks, chunks - 1]
    for before, k in zip([None, *order], order):
        from_relays(k)
        if before is not None:
            settle(before)
    settle(order[-1])


def tile_kernel(rows, cols, names_ref, cand_ref, scale_ref, out_ref, buffer, out_sem):
    blocks = cand_ref.shape[2]
    block_rows = cand_ref.shape[4]
    windows = cand_ref.shape[1]
    slots = out_ref.shape[1]
    halves = out_sem.shape[1]
    half = slots // halves
    r = lax.axis_index("row")
    c = lax.axis_index("col")
    home = HOP * cols + c

    def copy(i, h):
        part = pl.ds(h * half, half)
        return pltpu.make_async_copy(buffer.at[i, part], out_ref.at[i, part], out_sem.at[i, h])

    for i in range(blocks):
        local = [cand_ref[home, w, i].T for w in range(windows)]
        left = [
            jnp.broadcast_to(scale_ref[home, w, i : i + 1, :], (block_rows, block_rows)).T
            for w in range(windows)
        ]
        for k in range(0, slots, 2):
            found = []
            for q in (k, k + 1):
                name = names_ref[i, q]
                safe = jnp.maximum(name, 0)
                slab = safe // blocks
                distance = lax.rem(slab // cols - r + HOP + rows, rows)
                place = jnp.where(name >= 0, distance * cols + lax.rem(slab, cols), 0)
                found.append((name >= 0, place, lax.rem(safe, blocks)))
            for w in range(windows):
                right = jnp.concatenate([cand_ref[s, w, b] for _, s, b in found], axis=1)
                tiles = jnp.dot(local[w], right, preferred_element_type=jnp.float32)
                for n, (present, s, b) in enumerate(found):
                    tile = tiles[:, n * block_rows : (n + 1) * block_rows]
                    factor = jnp.where(present, scale_ref[s, w, pl.ds(b, 1), :], 0.0)
                    buffer[i, k + n, w] = (tile * left[w] * factor).astype(out_ref.dtype)
            if (k + 2) % half == 0:
                copy(i, (k + 2) // half - 1).start()
    for i in range(blocks):
        for h in range(halves):
            copy(i, h).wait()


def on_device(rows, cols, bold, gm_index, partners):
    windows, frames, sx, sy, sz = bold.shape
    voxels = sx * sy * sz
    count = gm_index.shape[0]
    blocks, slots = partners.shape
    block_rows = count // blocks
    slabs = (2 * HOP + 1) * cols
    bf16, f32 = jnp.bfloat16, jnp.float32
    n = max(PARTS) * frames // 16
    dma = pltpu.SemaphoreType.DMA
    in_hbm = [
        pltpu.with_memory_space_constraint(x, pltpu.HBM)
        for x in (gm_index.reshape(1, count), bold, partners)
    ]
    cand, scale, names = pl.pallas_call(
        functools.partial(panel_kernel, rows),
        out_shape=(
            jax.ShapeDtypeStruct((slabs, windows, blocks, frames, block_rows), bf16),
            jax.ShapeDtypeStruct((slabs, windows, blocks, block_rows), f32),
            jax.ShapeDtypeStruct(partners.shape, partners.dtype),
        ),
        in_specs=[pl.BlockSpec(memory_space=pltpu.HBM)] * 3,
        out_specs=(pl.BlockSpec(memory_space=pl.ANY),) * 3,
        scratch_shapes=[
            pltpu.VMEM((1, count), jnp.int32),
            pltpu.VMEM((windows, frames, sx, sy, sz), bf16),
            pltpu.VMEM((2 * sx + 2, frames, sy, sz), bf16),
            pltpu.VMEM((windows, sx, sy, sz), f32),
            pltpu.VMEM((2 * sx + 2, sy, sz), f32),
            pltpu.VMEM((2 * sx, sy, sz), f32),
            pltpu.VMEM((2 * sx, sy, sz), f32),
            pltpu.VMEM((2 * sx, sy, sz), f32),
            pltpu.VMEM((1, count), jnp.int32),
            pltpu.VMEM((2, voxels, count), bf16),
            pltpu.VMEM((2 * sx, n * sy, sz), f32),
            pltpu.VMEM((CHUNKS, 2 * sx, n, sz), f32),
            pltpu.VMEM((CHUNKS, 2 * sx, n, sz), f32),
            pltpu.VMEM((2, n, voxels), bf16),
            pltpu.VMEM((2, 1, count), f32),
            pltpu.VMEM((2, blocks, frames, block_rows), bf16),
            pltpu.VMEM((2, blocks, block_rows), f32),
            dma((6,)),
            dma((CHUNKS, 4)),
            dma((CHUNKS, 4)),
            dma((CHUNKS,)),
            dma((CHUNKS,)),
            dma((5,)),
            dma((5,)),
            dma((CHUNKS + 1, 2)),
            dma((CHUNKS + 1, 10)),
            dma((CHUNKS + 1, 2 * HOP + 1, 2)),
            dma((CHUNKS + 1, 2 * HOP + 1, 2)),
            dma((CHUNKS + 1, 2 * HOP + 1, 2)),
        ],
        compiler_params=pltpu.CompilerParams(
            collective_id=0, has_side_effects=True, vmem_limit_bytes=40 * 1024 * 1024
        ),
        name="panels",
    )(*in_hbm)
    out_shape = (blocks, slots, windows, block_rows, block_rows)
    return pl.pallas_call(
        functools.partial(tile_kernel, rows, cols),
        out_shape=jax.ShapeDtypeStruct(out_shape, bf16),
        in_specs=[pl.BlockSpec(memory_space=pltpu.SMEM)]
        + [pl.BlockSpec(memory_space=pltpu.VMEM)] * 2,
        out_specs=pl.BlockSpec(memory_space=pl.ANY),
        scratch_shapes=[pltpu.VMEM(out_shape, bf16), dma((blocks, 2))],
        compiler_params=pltpu.CompilerParams(vmem_limit_bytes=40 * 1024 * 1024),
        name="tiles",
    )(names, cand, scale)


def solution(mesh):
    rows, cols = mesh.shape["row"], mesh.shape["col"]
    in_specs = (P("subj", None, "row", "col", None), P(("row", "col")), P(("row", "col"), None))
    out_specs = P(("row", "col"), None, "subj", None, None)
    return jax.shard_map(
        functools.partial(on_device, rows, cols),
        mesh=mesh,
        in_specs=in_specs,
        out_specs=out_specs,
        check_vma=False,
    )
```
